32 devices in a mesh: groups: 2 (over y), theta: 16 (over z, x, core).
Axes of the slice: x: 2, y: 2, z: 4, core: 2. Of those that a mesh axis runs over, the one named last changes fastest.
Arguments:
- state_now: float32 [5, 2, 64, 256, 128], P(None, None, 'theta', 'groups'), parts along dimension 3, may hold values from -6 to 6
- state_prev: float32 [5, 2, 64, 256, 128], P(None, None, 'theta', 'groups'), parts along dimension 3, may hold values from -6 to 6
- eddy_visc: float32 [2, 64, 256, 128], P(None, 'theta', 'groups'), parts along dimension 2, may hold values from 0.01 to 0.2
- mean_flow: float32 [2, 4], replicated, may hold values from 0.5 to 1
- offset: int32 [2], P('groups'), parts along dimension 0, may hold values from 0 to 63
Outputs:
- field: float32 [5, 2, 64, 256, 128], P(None, None, 'theta', 'groups'), parts along dimension 3
The draws below stay inside these ranges and needn't reach their ends.
There are 2 independent parts, one for each index of `groups`. The reference program is written for one: setup_inputs(seed, part) draws one part's arguments, and reference() takes and returns one part's arrays. A program takes and returns all parts, laid end to end along the dimension named above; an argument that names none is the same for every part. Nothing has to cross between parts.
All inputs are finite; a program needn't handle non-finite values.
Results may differ from the reference program's by a relative error of at most 0.00002.
Values sent between devices are 32-bit elements; how exact they have to be, the bound alone decides.
A program may use at most 128 MiB of HBM per device.

```python
import math
import jax
import jax.numpy as jnp

R = 128
A = 128
ITERS = 2
NT = 64


def steps_of(key, extent, split, smallest, largest):
    factor_of, own = 1.0, jax.random.fold_in(key, 6)
    for axis_at, shards_of in split:
        steps = jnp.exp(jax.random.uniform(jax.random.fold_in(own, axis_at), (shards_of,), jnp.float32, smallest / len(split), largest / len(split)))
        factor_of = factor_of * jnp.repeat(steps, extent[axis_at] // shards_of).reshape([-1 if axis == axis_at else 1 for axis in range(len(extent))])
    return factor_of


def bell_draw(stream_key, extent, spread, bound, split=(), held_as=jnp.bfloat16):
    level = steps_of(stream_key, extent, split, -0.22, 0.18) if split else 1.0
    entries = jax.random.normal(stream_key, extent, jnp.float32) * spread * level
    return jnp.minimum(jnp.maximum(entries, -bound), bound).astype(held_as)


def setup_inputs(seed: int = 0, part: int = 0) -> dict:
    keys = jax.random.split(jax.random.key(seed), 6)
    part_keys = jax.random.split(jax.random.fold_in(keys[5], part), 6)
    return {
        "state_now": bell_draw(part_keys[0], (5, 2, NT, R, A), 1.0, 6.0, ((2, 16),), jnp.float32),
        "state_prev": bell_draw(part_keys[1], (5, 2, NT, R, A), 1.0, 6.0, ((2, 16),), jnp.float32),
        "eddy_visc": jnp.clip(jnp.exp(math.log(0.2) - 2.9957323 * jax.random.uniform(part_keys[2], (2, NT, R, A), jnp.float32) ** steps_of(part_keys[2], (2, NT, R, A), ((1, 16),), -0.2, 0.2)), 0.01, 0.2),
        "mean_flow": jnp.clip(jax.random.uniform(keys[3], (2, 4), jnp.float32, 0.5, 1.0), 0.5, 1.0),
        "offset": jax.random.randint(part_keys[4], (1,), 0, NT).astype(jnp.int32),
    }


PSEUDO_STEP = 0.2
PHYS_STEP = 1.0
SECTION_WEIGHTS = (0.6, 0.6, 1.0)


def operator_terms(padded, low_ghost, high_ghost, mean_row, eddy_row):
    center = padded[:, 1:-1]
    theta_diff = (padded[:, 2:] - padded[:, :-2]) * 0.5
    neighbours = padded[:, 2:] + padded[:, :-2]
    wall_sign = jnp.array([1.0, 1.0, 1.0, -1.0, 1.0], jnp.float32).reshape(5, 1, 1, 1)
    radial_pad = jnp.concatenate([center[:, :, :1] * wall_sign, center, center[:, :, -1:] * wall_sign], axis=2)
    radial_diff = (radial_pad[:, :, 2:] - radial_pad[:, :, :-2]) * 0.5
    neighbours = neighbours + radial_pad[:, :, 2:] + radial_pad[:, :, :-2]
    axial_pad = jnp.concatenate([low_ghost[..., None], center, high_ghost[..., None]], axis=3)
    axial_diff = (axial_pad[..., 2:] - axial_pad[..., :-2]) * 0.5
    neighbours = neighbours + axial_pad[..., 2:] + axial_pad[..., :-2]
    laplace = neighbours - 6.0 * center
    axial_speed = mean_row[0]
    swirl_speed = mean_row[1]
    density = mean_row[2]
    sound_speed = mean_row[3]
    convect = axial_speed * axial_diff + swirl_speed * theta_diff
    divergence = axial_diff[1] + theta_diff[2] + radial_diff[3]
    pressure_push = jnp.stack([density * divergence, axial_diff[4] / density, theta_diff[4] / density,
                               radial_diff[4] / density, density * sound_speed * sound_speed * divergence])
    return convect + pressure_push - eddy_row * laplace


def wrap_pad(row_field):
    return jnp.concatenate([row_field[:, -1:], row_field, row_field[:, :1]], axis=1)


def reference(state_now, state_prev, eddy_visc, mean_flow, offset):
    shift_cells = offset[0] % NT
    fixed_part = (state_prev - 4.0 * state_now) * (0.5 / PHYS_STEP)
    field = state_now
    for sweep in range(ITERS):
        start_field = field
        for weight in SECTION_WEIGHTS:
            rotor_row = field[:, 0]
            stator_row = field[:, 1]
            rotor_high = jnp.roll(stator_row[..., 0], -shift_cells, axis=1)
            stator_low = jnp.roll(rotor_row[..., -1], shift_cells, axis=1)
            rotor_terms = operator_terms(wrap_pad(rotor_row), jnp.zeros_like(rotor_high), rotor_high,
                                         mean_flow[0], eddy_visc[0])
            stator_terms = operator_terms(wrap_pad(stator_row), stator_low, stator_row[..., -1],
                                          mean_flow[1], eddy_visc[1])
            terms = jnp.stack([rotor_terms, stator_terms], axis=1)
            field = start_field - (weight * PSEUDO_STEP) * (terms + (1.5 / PHYS_STEP) * field + fixed_part)
    return field
```

```python
import functools
import jax
import jax.numpy as jnp
from jax import lax
from jax.experimental import pallas as pl
from jax.experimental.pallas import tpu as pltpu
from jax.sharding import PartitionSpec as P

ITERS = 2
PSEUDO_STEP = 0.2
PHYS_STEP = 1.0
SECTIONS = 3
WEIGHT_EARLY = 0.6
WEIGHT_LAST = 1.0
PAD = 8
CHUNK = 64
MESH = pl.DeviceIdType.MESH
FAR, NEAR = 0, 1


def slot_of(s):
    r = lax.rem(s, SECTIONS)
    it = lax.rem(lax.div(s, SECTIONS), 2)
    return r + it * (1 - 2 * r + 3 * lax.div(r, 2))


def kernel(
    count, cells, radial,
    mean_ref, offset_ref, now_ref, prev_ref, eddy_hbm,
    out_ref,
    fbuf, fixed, eddy_ref, stage, gcol, packed, edge_eddy, eddy_send, eddy_recv,
    choose, plane, plane_recv, picks, got,
    load_sem, hsend, hrecv, xsend, xrecv, gsend, grecv, esend, erecv,
):
    me = lax.axis_index("theta")
    core = lax.rem(me, 2)
    cross = lax.rem(lax.div(me, 2), 2)
    half = count // 2
    rank = lax.div(me, 4) * 2 + core
    total = ITERS * SECTIONS
    width = fbuf.shape[-1]
    used = 5 * cells
    window = 5 * (cells + 2)
    block = edge_eddy.shape[1]
    circle = cells * count
    f32 = jnp.float32

    def at(index):
        return {"theta": lax.rem(index + count, count)}

    def same_side(j):
        other = lax.rem(rank + j, half)
        return lax.div(other, 2) * 4 + cross * 2 + lax.rem(other, 2)

    partner = at(me + 2 - 4 * cross)

    def after(side):
        return core + side * (1 - 2 * core)

    def peer(side):
        return at(me + 2 * after(side) - 1)

    def edge_layer(side):
        return 1 + after(side) * (cells - 1)

    def halo_layer(side):
        return after(side) * (cells + 1)

    loads = [
        pltpu.make_async_copy(
            now_ref, fbuf.at[0, :, :, pl.ds(1, cells), pl.ds(PAD, radial)], load_sem.at[0]
        ),
        pltpu.make_async_copy(prev_ref, fixed, load_sem.at[1]),
        pltpu.make_async_copy(eddy_hbm, eddy_ref, load_sem.at[2]),
    ]
    for load in loads:
        load.start()

    barrier = pltpu.get_barrier_semaphore()
    greet = [peer(FAR), partner] + [at(same_side(j)) for j in range(1, half)]
    for device in greet:
        pl.semaphore_signal(barrier, inc=1, device_id=device, device_id_type=MESH)
    pl.semaphore_wait(barrier, len(greet))

    def halo(slot, row, side, piece, first=False):
        r0 = piece * CHUNK if isinstance(piece, int) else pl.multiple_of(piece * CHUNK, CHUNK)
        if first:
            source = now_ref.at[:, row, edge_layer(side) - 1, pl.ds(r0, CHUNK)]
        else:
            source = stage.at[row, side, :, pl.ds(r0, CHUNK)]
        return pltpu.make_async_remote_copy(
            src_ref=source,
            dst_ref=fbuf.at[slot, :, row, halo_layer(1 - side), pl.ds(PAD + r0, CHUNK)],
            send_sem=hsend.at[slot, row, side, piece],
            recv_sem=hrecv.at[slot, row, side, piece],
            device_id=peer(side),
            device_id_type=MESH,
        )

    def cross_plane(par):
        return pltpu.make_async_remote_copy(
            src_ref=plane.at[par],
            dst_ref=plane_recv.at[par],
            send_sem=xsend.at[par],
            recv_sem=xrecv.at[par],
            device_id=partner,
            device_id_type=MESH,
        )

    def spread(par, j):
        return pltpu.make_async_remote_copy(
            src_ref=picks.at[par, j],
            dst_ref=got.at[par, rank],
            send_sem=gsend.at[par, j],
            recv_sem=grecv.at[par, j],
            device_id=at(same_side(j)),
            device_id_type=MESH,
        )

    def edge_of(side):
        return pltpu.make_async_remote_copy(
            src_ref=eddy_send,
            dst_ref=eddy_recv.at[side],
            send_sem=esend.at[side],
            recv_sem=erecv.at[side],
            device_id=peer(side),
            device_id_type=MESH,
        )

    for row in range(2):
        for side in (FAR, NEAR):
            for piece in range(radial // CHUNK):
                halo(0, row, side, piece, True).start()

    inverse = [(1.0 / jnp.full((8, width), mean_ref[row, 2], f32))[0, 0] for row in range(2)]
    shift = lax.rem(offset_ref[0], circle)
    start = [lax.rem(2 * circle - shift - 1, circle), lax.rem(circle + shift - 1, circle)]
    sector = [lax.div(value, cells) for value in start]
    within = [lax.rem(value, cells) for value in start]

    rows = lax.broadcasted_iota(jnp.int32, (2 * used, width), 0)
    is_stator = rows >= used
    is_end = lax.rem(lax.div(rows, 5), cells) == cells - 1

    def whether(target, part):
        apart = lax.rem(me - target - sector[part] + 2 * count, count)
        early = jnp.where(apart < 2, 1, 0)
        late = jnp.where(apart == 1, 1, jnp.where(apart == 2, 1, 0))
        return early, jnp.where(within[part] == cells - 1, late, early)

    for j in range(half):
        ends, rest = zip(*[whether(same_side(j), part) for part in range(2)])
        choose[j] = jnp.where(
            is_stator,
            jnp.where(is_end, ends[1], rest[1]),
            jnp.where(is_end, ends[0], rest[0]),
        )

    lane = lax.broadcasted_iota(jnp.int32, (CHUNK, width), 1)
    is_first = lane == 0
    is_last = lane == width - 1
    edge_lane = (width - 1, 0)
    edge_mask = (is_last, is_first)

    def place(acc, value, row, j):
        return jnp.where(lane == j, pltpu.roll(value, (j - edge_lane[row]) % width, 1), acc)

    def ghosts(slot):
        for row in range(2):
            for t in range(1, cells + 1):
                low = [fbuf[slot, c, row, t, pl.ds(PAD, 1), :] for c in range(5)]
                high = [fbuf[slot, c, row, t, pl.ds(PAD + radial - 1, 1), :] for c in range(5)]
                for c in range(5):
                    sign = -1.0 if c == 3 else 1.0
                    fbuf[slot, c, row, t, pl.ds(PAD - 1, 1), :] = sign * low[c]
                    fbuf[slot, c, row, t, pl.ds(PAD + radial, 1), :] = sign * high[c]

    def send_planes(par, own=None):
        lines = packed[...].T[: 2 * used]
        plane[par] = lines if own is None else lines + own
        cross_plane(par).start()

    def answer(par):
        cross_plane(par).wait()
        mine = plane[par]
        theirs = plane_recv[par]
        for j in range(half):
            picked = jnp.where(choose[j] > 0, mine, theirs)
            if j == 0:
                got[par, rank] = picked
            else:
                picks[par, j] = picked
                spread(par, j).start()

    def facing(par, part):
        parts = []
        for n in range(3):
            where = lax.rem(me + sector[part] + n, count)
            index = lax.div(where, 4) * 2 + lax.rem(where, 2)
            value = got[par, 0]
            for m in range(1, half):
                value = jnp.where(index == m, got[par, m], value)
            parts.append(value[part * used : (part + 1) * used])
        joined = jnp.concatenate(parts, axis=0)
        out = joined[:window]
        for m in range(1, cells):
            out = jnp.where(within[part] == m, joined[5 * m : 5 * m + window], out)
        return out

    component = lax.rem(lax.broadcasted_iota(jnp.int32, (window, width), 0), 5)

    def columns_of(par, k):
        pieces = []
        own = []
        for row in range(2):
            ghost = facing(par, 1 - row)
            half_k = (0.5 if row == 0 else -0.5) * k
            density, sound = mean_ref[row, 2], mean_ref[row, 3]
            up1 = jnp.concatenate([ghost[1:], ghost[:1]], axis=0)
            up3 = jnp.concatenate([ghost[3:], ghost[:3]], axis=0)
            down3 = jnp.concatenate([ghost[-3:], ghost[:-3]], axis=0)
            delta = (edge_eddy[row][:window] * k - mean_ref[row, 0] * half_k) * ghost
            push = jnp.where(
                component == 0,
                (density * half_k) * up1,
                jnp.where(
                    component == 1,
                    (inverse[row] * half_k) * up3,
                    jnp.where(component == 4, (density * sound * sound * half_k) * down3, 0.0),
                ),
            )
            delta = delta - push
            own.append(delta[5 : 5 + used])
            pieces.append(delta)
            pieces.append(jnp.zeros((block - window, width), f32))
        pieces.append(jnp.zeros((width - 2 * block, width), f32))
        gcol[par] = jnp.concatenate(pieces, axis=0).T
        return jnp.concatenate(own, axis=0)

    def patch_piece(slot, row, t, i, par):
        r0 = pl.multiple_of(i * CHUNK, CHUNK)
        columns = gcol[par, pl.ds(r0, CHUNK), :]
        new = []
        for c in range(5):
            amount = edge_lane[row] - row * block - t * 5 - c
            amount = amount % width if isinstance(t, int) else lax.rem(amount + 2 * width, width)
            moved = pltpu.roll(columns, amount, 1)
            value = fbuf[slot, c, row, t, pl.ds(r0 + PAD, CHUNK), :]
            new.append(value + jnp.where(edge_mask[row], moved, 0.0))
        for c in range(5):
            fbuf[slot, c, row, t, pl.ds(r0 + PAD, CHUNK), :] = new[c]

    def patch(slot, layers, par):
        def body(i, carry):
            for row, t in layers:
                patch_piece(slot, row, t, i, par)
            return carry

        lax.fori_loop(0, radial // CHUNK, body, 0)

    def pack(slot, layers, fresh):
        def body(i, carry):
            r0 = pl.multiple_of(i * CHUNK, CHUNK)
            acc = jnp.zeros((CHUNK, width), f32) if fresh else packed[pl.ds(r0, CHUNK), :]
            for row, t in layers:
                for c in range(5):
                    value = fbuf[slot, c, row, t, pl.ds(r0 + PAD, CHUNK), :]
                    acc = place(acc, value, row, row * used + (t - 1) * 5 + c)
            packed[pl.ds(r0, CHUNK), :] = acc
            return carry

        lax.fori_loop(0, radial // CHUNK, body, 0)

    def layer_piece(cur, new, origin, row, t, k, i, side=None):
        half_u = mean_ref[row, 0] * (0.5 * k)
        half_v = mean_ref[row, 1] * (0.5 * k)
        push_rho = mean_ref[row, 2] * (0.5 * k)
        push_inv = inverse[row] * (0.5 * k)
        push_p = mean_ref[row, 2] * mean_ref[row, 3] * mean_ref[row, 3] * (0.5 * k)

        r0 = pl.multiple_of(i * CHUNK, CHUNK)
        ke = eddy_ref[row, t - 1, pl.ds(r0, CHUNK), :] * k
        cf = ke * 6.0 + (1.5 / PHYS_STEP) * k
        partial = []
        extra = {}
        div = None
        for c in range(5):
            f = fbuf[cur, c, row, t, pl.ds(r0 + PAD, CHUNK), :]
            rm = fbuf[cur, c, row, t, pl.ds(r0 + (PAD - 1), CHUNK), :]
            rp = fbuf[cur, c, row, t, pl.ds(r0 + (PAD + 1), CHUNK), :]
            tm = fbuf[cur, c, row, t - 1, pl.ds(r0 + PAD, CHUNK), :]
            tp = fbuf[cur, c, row, t + 1, pl.ds(r0 + PAD, CHUNK), :]
            am = jnp.where(is_first, 0.0, pltpu.roll(f, 1, 1))
            ap = jnp.where(is_last, 0.0 if row == 0 else f, pltpu.roll(f, width - 1, 1))
            da = ap - am
            dt = tp - tm
            around = (ap + am) + (tp + tm) + (rp + rm)
            value = (
                fbuf[origin, c, row, t, pl.ds(r0 + PAD, CHUNK), :]
                - k * fixed[c, row, t - 1, pl.ds(r0, CHUNK), :]
                - cf * f
                + ke * around
                - half_u * da
                - half_v * dt
            )
            if c == 1:
                div = da
            elif c == 2:
                div = div + dt
            elif c == 3:
                div = div + (rp - rm)
            elif c == 4:
                extra = {1: da, 2: dt, 3: rp - rm}
            partial.append(value)
        for c in range(5):
            if c == 0:
                value = partial[0] - push_rho * div
            elif c == 4:
                value = partial[4] - push_p * div
            else:
                value = partial[c] - push_inv * extra[c]
            fbuf[new, c, row, t, pl.ds(r0 + PAD, CHUNK), :] = value
            if side is not None:
                stage[row, side, c, pl.ds(r0, CHUNK), :] = value

    def layer(cur, new, origin, row, t, k):
        def body(i, carry):
            layer_piece(cur, new, origin, row, t, k, i)
            return carry

        lax.fori_loop(0, radial // CHUNK, body, 0)

    loads[2].wait()

    def eddy_columns(i, carry):
        r0 = pl.multiple_of(i * CHUNK, CHUNK)
        acc = jnp.zeros((CHUNK, width), f32)
        for row in range(2):
            for t in range(cells):
                acc = place(acc, eddy_ref[row, t, pl.ds(r0, CHUNK), :], row, row * cells + t)
        packed[pl.ds(r0, CHUNK), :] = acc
        return carry

    lax.fori_loop(0, radial // CHUNK, eddy_columns, 0)
    eddy_send[...] = packed[...].T[: 2 * cells]
    for side in (FAR, NEAR):
        edge_of(side).start()
    loads[0].wait()
    rotor = [(0, t) for t in range(1, cells + 1)]
    stator_inner = [(1, t) for t in range(2, cells)]
    stator_edges = [(1, t) for t in sorted({1, cells})]
    pack(0, rotor + stator_inner + stator_edges, True)
    send_planes(0)
    ghosts(0)
    gcol[...] = jnp.zeros_like(gcol)
    loads[1].wait()

    def prepare(t, carry):
        for c in range(5):
            for row in range(2):
                fixed[c, row, t] = (0.5 / PHYS_STEP) * fixed[c, row, t] - (
                    2.0 / PHYS_STEP
                ) * fbuf[0, c, row, t + 1, pl.ds(PAD, radial), :]
        return carry

    lax.fori_loop(0, cells, prepare, 0)
    def join_eddy():
        for side in (FAR, NEAR):
            edge_of(side).wait()
        left = jnp.where(core == 0, eddy_recv[FAR], eddy_recv[NEAR])
        right = jnp.where(core == 0, eddy_recv[NEAR], eddy_recv[FAR])
        for row in range(2):
            own = eddy_send[...]
            line = [left[(row + 1) * cells - 1 : (row + 1) * cells]]
            line += [own[row * cells + t : row * cells + t + 1] for t in range(cells)]
            line += [right[row * cells : row * cells + 1]]
            edge_eddy[row] = jnp.concatenate(
                [jnp.broadcast_to(value, (5, width)) for value in line]
                + [jnp.zeros((block - window, width), f32)],
                axis=0,
            )

    def stores(chosen):
        pieces = [(0, 1, cells), (1, 2, cells - 2), (1, 1, 1), (1, cells, 1)]
        return [
            pltpu.make_async_copy(
                fbuf.at[0, :, row, pl.ds(t, n), pl.ds(PAD, radial)],
                out_ref.at[:, row, pl.ds(t - 1, n)],
                load_sem.at[index],
            )
            for index, (row, t, n) in enumerate(pieces)
            if index in chosen
        ]

    def section(s, carry):
        cur = slot_of(s)
        new = slot_of(s + 1)
        origin = lax.div(s, SECTIONS)
        par = lax.rem(s, 2)
        k = jnp.where(
            lax.rem(s, SECTIONS) == SECTIONS - 1,
            f32(WEIGHT_LAST * PSEUDO_STEP),
            f32(WEIGHT_EARLY * PSEUDO_STEP),
        )
        final = lax.div(s, total - 1)

        def edges(row):
            for n in range(2):
                side = n + final * (1 - 2 * n)

                def one(i, carry):
                    halo(cur, row, side, i).wait()
                    patch_piece(cur, row, halo_layer(side), i, 1 - par)
                    layer_piece(cur, new, origin, row, edge_layer(side), k, i, side)

                    @pl.when(s < total - 1)
                    def _():
                        halo(new, row, side, i).start()

                    return carry

                lax.fori_loop(0, radial // CHUNK, one, 0)

        edges(0)
        for row in range(2):

            def inner(t, carry):
                layer(cur, new, origin, row, t, k)
                return carry

            lax.fori_loop(2, cells, inner, 0)

        answer(par)

        def take():
            for j in range(1, half):
                spread(par, j).wait()

            @pl.when(s == 0)
            def _():
                join_eddy()

            return columns_of(par, k)

        @pl.when(s < total - 1)
        def _():
            pack(new, rotor + stator_inner, True)

        @pl.when(s == total - 1)
        def _():
            take()
            patch(new, rotor + stator_inner, par)
            for store in stores((0, 1)):
                store.start()

        edges(1)

        @pl.when(s < total - 1)
        def _():
            pack(new, stator_edges, False)
            send_planes(1 - par, take())
            patch(new, rotor + stator_inner + stator_edges, par)
            ghosts(new)

        return carry

    lax.fori_loop(0, total, section, 0)
    for n, place_of in enumerate(stator_edges):
        patch(0, [place_of], (total - 1) % 2)
        stores((2 + n,))[0].start()
    for store in stores(range(4)):
        store.wait()


def per_device(state_now, state_prev, eddy_visc, mean_flow, offset):
    _, _, cells, radial, width = state_now.shape
    count = lax.axis_size("theta")
    half = count // 2
    block = -(-5 * (cells + 2) // 8) * 8
    used = 5 * cells
    f32 = jnp.float32
    hbm = pl.BlockSpec(memory_space=pltpu.HBM)
    smem = pl.BlockSpec(memory_space=pltpu.SMEM)
    return pl.pallas_call(
        functools.partial(kernel, count, cells, radial),
        out_shape=jax.ShapeDtypeStruct(state_now.shape, f32),
        in_specs=[smem, smem, hbm, hbm, hbm],
        out_specs=pl.BlockSpec(memory_space=pltpu.VMEM),
        scratch_shapes=[
            pltpu.VMEM((3, 5, 2, cells + 2, radial + 2 * PAD, width), f32),
            pltpu.VMEM((5, 2, cells, radial, width), f32),
            pltpu.VMEM((2, cells, radial, width), f32),
            pltpu.VMEM((2, 2, 5, radial, width), f32),
            pltpu.VMEM((2, radial, width), f32),
            pltpu.VMEM((radial, width), f32),
            pltpu.VMEM((2, block, radial), f32),
            pltpu.VMEM((2 * cells, radial), f32),
            pltpu.VMEM((2, 2 * cells, radial), f32),
            pltpu.VMEM((half, 2 * used, radial), jnp.int32),
            pltpu.VMEM((2, 2 * used, radial), f32),
            pltpu.VMEM((2, 2 * used, radial), f32),
            pltpu.VMEM((2, half, 2 * used, radial), f32),
            pltpu.VMEM((2, half, 2 * used, radial), f32),
            pltpu.SemaphoreType.DMA((4,)),
            pltpu.SemaphoreType.DMA((3, 2, 2, radial // CHUNK)),
            pltpu.SemaphoreType.DMA((3, 2, 2, radial // CHUNK)),
            pltpu.SemaphoreType.DMA((2,)),
            pltpu.SemaphoreType.DMA((2,)),
            pltpu.SemaphoreType.DMA((2, half)),
            pltpu.SemaphoreType.DMA((2, half)),
            pltpu.SemaphoreType.DMA((2,)),
            pltpu.SemaphoreType.DMA((2,)),
        ],
        compiler_params=pltpu.CompilerParams(
            collective_id=0, has_side_effects=True, vmem_limit_bytes=50 * 1024 * 1024
        ),
    )(mean_flow, offset, state_now, state_prev, eddy_visc)


def solution(mesh):
    placed = (
        P(None, None, "theta", "groups", None),
        P(None, None, "theta", "groups", None),
        P(None, "theta", "groups", None),
        P(),
        P("groups"),
    )
    return jax.shard_map(
        per_device,
        mesh=mesh,
        in_specs=placed,
        out_specs=P(None, None, "theta", "groups", None),
        check_vma=False,
    )
```

```python
import functools
import jax
import jax.numpy as jnp
from jax import lax
from jax.experimental import pallas as pl
from jax.experimental.pallas import tpu as pltpu
from jax.sharding import PartitionSpec as P

ITERS = 2
PSEUDO_STEP = 0.2
PHYS_STEP = 1.0
SECTIONS = 3
WEIGHT_EARLY = 0.6
WEIGHT_LAST = 1.0
PAD = 8
CHUNK = 64
MESH = pl.DeviceIdType.MESH
FAR, NEAR = 0, 1


def slot_of(s):
    r = lax.rem(s, SECTIONS)
    it = lax.rem(lax.div(s, SECTIONS), 2)
    return r + it * (1 - 2 * r + 3 * lax.div(r, 2))


def kernel(
    count, cells, radial,
    mean_ref, offset_ref, now_ref, prev_ref, eddy_hbm,
    out_ref,
    fbuf, fixed, eddy_ref, stage, gcol, packed, edge_eddy, eddy_send, eddy_recv,
    choose, plane, plane_recv, picks, got,
    load_sem, hsend, hrecv, xsend, xrecv, gsend, grecv, esend, erecv,
):
    me = lax.axis_index("theta")
    core = lax.rem(me, 2)
    cross = lax.rem(lax.div(me, 2), 2)
    half = count // 2
    rank = lax.div(me, 4) * 2 + core
    total = ITERS * SECTIONS
    width = fbuf.shape[-1]
    used = 5 * cells
    window = 5 * (cells + 2)
    block = edge_eddy.shape[1]
    circle = cells * count
    f32 = jnp.float32

    def at(index):
        return {"theta": lax.rem(index + count, count)}

    def same_side(j):
        other = lax.rem(rank + j, half)
        return lax.div(other, 2) * 4 + cross * 2 + lax.rem(other, 2)

    partner = at(me + 2 - 4 * cross)

    def after(side):
        return core + side * (1 - 2 * core)

    def peer(side):
        return at(me + 2 * after(side) - 1)

    def edge_layer(side):
        return 1 + after(side) * (cells - 1)

    def halo_layer(side):
        return after(side) * (cells + 1)

    loads = [
        pltpu.make_async_copy(
            now_ref, fbuf.at[0, :, :, pl.ds(1, cells), pl.ds(PAD, radial)], load_sem.at[0]
        ),
        pltpu.make_async_copy(prev_ref, fixed, load_sem.at[1]),
        pltpu.make_async_copy(eddy_hbm, eddy_ref, load_sem.at[2]),
    ]
    for load in loads:
        load.start()

    barrier = pltpu.get_barrier_semaphore()
    greet = [peer(FAR), partner] + [at(same_side(j)) for j in range(1, half)]
    for device in greet:
        pl.semaphore_signal(barrier, inc=1, device_id=device, device_id_type=MESH)
    pl.semaphore_wait(barrier, len(greet))

    def halo(slot, row, side, piece, first=False):
        r0 = piece * CHUNK if isinstance(piece, int) else pl.multiple_of(piece * CHUNK, CHUNK)
        if first:
            source = now_ref.at[:, row, edge_layer(side) - 1, pl.ds(r0, CHUNK)]
        else:
            source = stage.at[row, side, :, pl.ds(r0, CHUNK)]
        return pltpu.make_async_remote_copy(
            src_ref=source,
            dst_ref=fbuf.at[slot, :, row, halo_layer(1 - side), pl.ds(PAD + r0, CHUNK)],
            send_sem=hsend.at[slot, row, side, piece],
            recv_sem=hrecv.at[slot, row, side, piece],
            device_id=peer(side),
            device_id_type=MESH,
        )

    def cross_plane(par):
        return pltpu.make_async_remote_copy(
            src_ref=plane.at[par],
            dst_ref=plane_recv.at[par],
            send_sem=xsend.at[par],
            recv_sem=xrecv.at[par],
            device_id=partner,
            device_id_type=MESH,
        )

    def spread(par, j):
        return pltpu.make_async_remote_copy(
            src_ref=picks.at[par, j],
            dst_ref=got.at[par, rank],
            send_sem=gsend.at[par, j],
            recv_sem=grecv.at[par, j],
            device_id=at(same_side(j)),
            device_id_type=MESH,
        )

    def edge_of(side):
        return pltpu.make_async_remote_copy(
            src_ref=eddy_send,
            dst_ref=eddy_recv.at[side],
            send_sem=esend.at[side],
            recv_sem=erecv.at[side],
            device_id=peer(side),
            device_id_type=MESH,
        )

    for row in range(2):
        for side in (FAR, NEAR):
            for piece in range(radial // CHUNK):
                halo(0, row, side, piece, True).start()

    inverse = [(1.0 / jnp.full((8, width), mean_ref[row, 2], f32))[0, 0] for row in range(2)]
    shift = lax.rem(offset_ref[0], circle)
    start = [lax.rem(2 * circle - shift - 1, circle), lax.rem(circle + shift - 1, circle)]
    sector = [lax.div(value, cells) for value in start]
    within = [lax.rem(value, cells) for value in start]

    rows = lax.broadcasted_iota(jnp.int32, (2 * used, width), 0)
    is_stator = rows >= used
    is_end = lax.rem(lax.div(rows, 5), cells) == cells - 1

    def whether(target, part):
        apart = lax.rem(me - target - sector[part] + 2 * count, count)
        early = jnp.where(apart < 2, 1, 0)
        late = jnp.where(apart == 1, 1, jnp.where(apart == 2, 1, 0))
        return early, jnp.where(within[part] == cells - 1, late, early)

    for j in range(half):
        ends, rest = zip(*[whether(same_side(j), part) for part in range(2)])
        choose[j] = jnp.where(
            is_stator,
            jnp.where(is_end, ends[1], rest[1]),
            jnp.where(is_end, ends[0], rest[0]),
        )

    lane = lax.broadcasted_iota(jnp.int32, (CHUNK, width), 1)
    is_first = lane == 0
    is_last = lane == width - 1
    edge_lane = (width - 1, 0)
    edge_mask = (is_last, is_first)

    def place(acc, value, row, j):
        return jnp.where(lane == j, pltpu.roll(value, (j - edge_lane[row]) % width, 1), acc)

    def ghosts(slot):
        for row in range(2):
            for t in range(1, cells + 1):
                low = [fbuf[slot, c, row, t, pl.ds(PAD, 1), :] for c in range(5)]
                high = [fbuf[slot, c, row, t, pl.ds(PAD + radial - 1, 1), :] for c in range(5)]
                for c in range(5):
                    sign = -1.0 if c == 3 else 1.0
                    fbuf[slot, c, row, t, pl.ds(PAD - 1, 1), :] = sign * low[c]
                    fbuf[slot, c, row, t, pl.ds(PAD + radial, 1), :] = sign * high[c]

    def send_planes(par, own=None):
        lines = packed[...].T[: 2 * used]
        plane[par] = lines if own is None else lines + own
        cross_plane(par).start()

    def answer(par):
        cross_plane(par).wait()
        mine = plane[par]
        theirs = plane_recv[par]
        for j in range(half):
            picked = jnp.where(choose[j] > 0, mine, theirs)
            if j == 0:
                got[par, rank] = picked
            else:
                picks[par, j] = picked
                spread(par, j).start()

    def facing(par, part):
        parts = []
        for n in range(3):
            where = lax.rem(me + sector[part] + n, count)
            index = lax.div(where, 4) * 2 + lax.rem(where, 2)
            value = got[par, 0]
            for m in range(1, half):
                value = jnp.where(index == m, got[par, m], value)
            parts.append(value[part * used : (part + 1) * used])
        joined = jnp.concatenate(parts, axis=0)
        out = joined[:window]
        for m in range(1, cells):
            out = jnp.where(within[part] == m, joined[5 * m : 5 * m + window], out)
        return out

    component = lax.rem(lax.broadcasted_iota(jnp.int32, (window, width), 0), 5)

    def columns_of(par, k):
        pieces = []
        own = []
        for row in range(2):
            ghost = facing(par, 1 - row)
            half_k = (0.5 if row == 0 else -0.5) * k
            density, sound = mean_ref[row, 2], mean_ref[row, 3]
            up1 = jnp.concatenate([ghost[1:], ghost[:1]], axis=0)
            up3 = jnp.concatenate([ghost[3:], ghost[:3]], axis=0)
            down3 = jnp.concatenate([ghost[-3:], ghost[:-3]], axis=0)
            delta = (edge_eddy[row][:window] * k - mean_ref[row, 0] * half_k) * ghost
            push = jnp.where(
                component == 0,
                (density * half_k) * up1,
                jnp.where(
                    component == 1,
                    (inverse[row] * half_k) * up3,
                    jnp.where(component == 4, (density * sound * sound * half_k) * down3, 0.0),
                ),
            )
            delta = delta - push
            own.append(delta[5 : 5 + used])
            pieces.append(delta)
            pieces.append(jnp.zeros((block - window, width), f32))
        pieces.append(jnp.zeros((width - 2 * block, width), f32))
        gcol[par] = jnp.concatenate(pieces, axis=0).T
        return jnp.concatenate(own, axis=0)

    def patch_piece(slot, row, t, i, par):
        r0 = pl.multiple_of(i * CHUNK, CHUNK)
        columns = gcol[par, pl.ds(r0, CHUNK), :]
        new = []
        for c in range(5):
            amount = edge_lane[row] - row * block - t * 5 - c
            amount = amount % width if isinstance(t, int) else lax.rem(amount + 2 * width, width)
            moved = pltpu.roll(columns, amount, 1)
            value = fbuf[slot, c, row, t, pl.ds(r0 + PAD, CHUNK), :]
            new.append(value + jnp.where(edge_mask[row], moved, 0.0))
        for c in range(5):
            fbuf[slot, c, row, t, pl.ds(r0 + PAD, CHUNK), :] = new[c]

    def patch(slot, layers, par):
        def body(i, carry):
            for row, t in layers:
                patch_piece(slot, row, t, i, par)
            return carry

        lax.fori_loop(0, radial // CHUNK, body, 0)

    def pack(slot, layers, fresh):
        def body(i, carry):
            r0 = pl.multiple_of(i * CHUNK, CHUNK)
            acc = jnp.zeros((CHUNK, width), f32) if fresh else packed[pl.ds(r0, CHUNK), :]
            for row, t in layers:
                for c in range(5):
                    value = fbuf[slot, c, row, t, pl.ds(r0 + PAD, CHUNK), :]
                    acc = place(acc, value, row, row * used + (t - 1) * 5 + c)
            packed[pl.ds(r0, CHUNK), :] = acc
            return carry

        lax.fori_loop(0, radial // CHUNK, body, 0)

    def layer_piece(cur, new, origin, row, t, k, i, side=None):
        half_u = mean_ref[row, 0] * (0.5 * k)
        half_v = mean_ref[row, 1] * (0.5 * k)
        push_rho = mean_ref[row, 2] * (0.5 * k)
        push_inv = inverse[row] * (0.5 * k)
        push_p = mean_ref[row, 2] * mean_ref[row, 3] * mean_ref[row, 3] * (0.5 * k)

        r0 = pl.multiple_of(i * CHUNK, CHUNK)
        ke = eddy_ref[row, t - 1, pl.ds(r0, CHUNK), :] * k
        cf = ke * 6.0 + (1.5 / PHYS_STEP) * k
        partial = []
        extra = {}
        div = None
        for c in range(5):
            f = fbuf[cur, c, row, t, pl.ds(r0 + PAD, CHUNK), :]
            rm = fbuf[cur, c, row, t, pl.ds(r0 + (PAD - 1), CHUNK), :]
            rp = fbuf[cur, c, row, t, pl.ds(r0 + (PAD + 1), CHUNK), :]
            tm = fbuf[cur, c, row, t - 1, pl.ds(r0 + PAD, CHUNK), :]
            tp = fbuf[cur, c, row, t + 1, pl.ds(r0 + PAD, CHUNK), :]
            am = jnp.where(is_first, 0.0, pltpu.roll(f, 1, 1))
            ap = jnp.where(is_last, 0.0 if row == 0 else f, pltpu.roll(f, width - 1, 1))
            da = ap - am
            dt = tp - tm
            around = (ap + am) + (tp + tm) + (rp + rm)
            value = (
                fbuf[origin, c, row, t, pl.ds(r0 + PAD, CHUNK), :]
                - k * fixed[c, row, t - 1, pl.ds(r0, CHUNK), :]
                - cf * f
                + ke * around
                - half_u * da
                - half_v * dt
            )
            if c == 1:
                div = da
            elif c == 2:
                div = div + dt
            elif c == 3:
                div = div + (rp - rm)
            elif c == 4:
                extra = {1: da, 2: dt, 3: rp - rm}
            partial.append(value)
        for c in range(5):
            if c == 0:
                value = partial[0] - push_rho * div
            elif c == 4:
                value = partial[4] - push_p * div
            else:
                value = partial[c] - push_inv * extra[c]
            fbuf[new, c, row, t, pl.ds(r0 + PAD, CHUNK), :] = value
            if side is not None:
                stage[row, side, c, pl.ds(r0, CHUNK), :] = value

    def layer(cur, new, origin, row, t, k):
        def body(i, carry):
            layer_piece(cur, new, origin, row, t, k, i)
            return carry

        lax.fori_loop(0, radial // CHUNK, body, 0)

    loads[2].wait()

    def eddy_columns(i, carry):
        r0 = pl.multiple_of(i * CHUNK, CHUNK)
        acc = jnp.zeros((CHUNK, width), f32)
        for row in range(2):
            for t in range(cells):
                acc = place(acc, eddy_ref[row, t, pl.ds(r0, CHUNK), :], row, row * cells + t)
        packed[pl.ds(r0, CHUNK), :] = acc
        return carry

    lax.fori_loop(0, radial // CHUNK, eddy_columns, 0)
    eddy_send[...] = packed[...].T[: 2 * cells]
    for side in (FAR, NEAR):
        edge_of(side).start()
    loads[0].wait()
    rotor = [(0, t) for t in range(1, cells + 1)]
    stator_inner = [(1, t) for t in range(2, cells)]
    stator_edges = [(1, t) for t in sorted({1, cells})]
    pack(0, rotor + stator_inner + stator_edges, True)
    send_planes(0)
    ghosts(0)
    gcol[...] = jnp.zeros_like(gcol)
    loads[1].wait()

    def prepare(t, carry):
        for c in range(5):
            for row in range(2):
                fixed[c, row, t] = (0.5 / PHYS_STEP) * fixed[c, row, t] - (
                    2.0 / PHYS_STEP
                ) * fbuf[0, c, row, t + 1, pl.ds(PAD, radial), :]
        return carry

    lax.fori_loop(0, cells, prepare, 0)
    def join_eddy():
        for side in (FAR, NEAR):
            edge_of(side).wait()
        left = jnp.where(core == 0, eddy_recv[FAR], eddy_recv[NEAR])
        right = jnp.where(core == 0, eddy_recv[NEAR], eddy_recv[FAR])
        for row in range(2):
            own = eddy_send[...]
            line = [left[(row + 1) * cells - 1 : (row + 1) * cells]]
            line += [own[row * cells + t : row * cells + t + 1] for t in range(cells)]
            line += [right[row * cells : row * cells + 1]]
            edge_eddy[row] = jnp.concatenate(
                [jnp.broadcast_to(value, (5, width)) for value in line]
                + [jnp.zeros((block - window, width), f32)],
                axis=0,
            )

    def stores(chosen):
        pieces = [(0, 1, cells), (1, 2, cells - 2), (1, 1, 1), (1, cells, 1)]
        return [
            pltpu.make_async_copy(
                fbuf.at[0, :, row, pl.ds(t, n), pl.ds(PAD, radial)],
                out_ref.at[:, row, pl.ds(t - 1, n)],
                load_sem.at[index],
            )
            for index, (row, t, n) in enumerate(pieces)
            if index in chosen
        ]

    def section(s, carry):
        cur = slot_of(s)
        new = slot_of(s + 1)
        origin = lax.div(s, SECTIONS)
        par = lax.rem(s, 2)
        k = jnp.where(
            lax.rem(s, SECTIONS) == SECTIONS - 1,
            f32(WEIGHT_LAST * PSEUDO_STEP),
            f32(WEIGHT_EARLY * PSEUDO_STEP),
        )
        final = lax.div(s, total - 1)

        def edges(row):
            for n in range(2):
                side = n + final * (1 - 2 * n)

                def one(i, carry):
                    halo(cur, row, side, i).wait()
                    patch_piece(cur, row, halo_layer(side), i, 1 - par)
                    layer_piece(cur, new, origin, row, edge_layer(side), k, i, side)

                    @pl.when(s < total - 1)
                    def _():
                        halo(new, row, side, i).start()

                    return carry

                lax.fori_loop(0, radial // CHUNK, one, 0)

        def inside(row):
            def inner(t, carry):
                layer(cur, new, origin, row, t, k)
                return carry

            lax.fori_loop(2, cells, inner, 0)

        def take():
            for j in range(1, half):
                spread(par, j).wait()

            @pl.when(s == 0)
            def _():
                join_eddy()

            return columns_of(par, k)

        edges(0)
        answer(par)
        inside(0)
        pack(new, rotor, True)

        @pl.when(s == total - 1)
        def _():
            inside(1)
            take()
            patch(new, rotor + stator_inner, par)
            for store in stores((0, 1)):
                store.start()

        edges(1)

        @pl.when(s < total - 1)
        def _():
            inside(1)
            pack(new, stator_inner + stator_edges, False)
            send_planes(1 - par, take())
            patch(new, rotor + stator_inner + stator_edges, par)
            ghosts(new)

        return carry

    lax.fori_loop(0, total, section, 0)
    for n, place_of in enumerate(stator_edges):
        patch(0, [place_of], (total - 1) % 2)
        stores((2 + n,))[0].start()
    for store in stores(range(4)):
        store.wait()


def per_device(state_now, state_prev, eddy_visc, mean_flow, offset):
    _, _, cells, radial, width = state_now.shape
    count = lax.axis_size("theta")
    half = count // 2
    block = -(-5 * (cells + 2) // 8) * 8
    used = 5 * cells
    f32 = jnp.float32
    hbm = pl.BlockSpec(memory_space=pltpu.HBM)
    smem = pl.BlockSpec(memory_space=pltpu.SMEM)
    return pl.pallas_call(
        functools.partial(kernel, count, cells, radial),
        out_shape=jax.ShapeDtypeStruct(state_now.shape, f32),
        in_specs=[smem, smem, hbm, hbm, hbm],
        out_specs=pl.BlockSpec(memory_space=pltpu.VMEM),
        scratch_shapes=[
            pltpu.VMEM((3, 5, 2, cells + 2, radial + 2 * PAD, width), f32),
            pltpu.VMEM((5, 2, cells, radial, width), f32),
            pltpu.VMEM((2, cells, radial, width), f32),
            pltpu.VMEM((2, 2, 5, radial, width), f32),
            pltpu.VMEM((2, radial, width), f32),
            pltpu.VMEM((radial, width), f32),
            pltpu.VMEM((2, block, radial), f32),
            pltpu.VMEM((2 * cells, radial), f32),
            pltpu.VMEM((2, 2 * cells, radial), f32),
            pltpu.VMEM((half, 2 * used, radial), jnp.int32),
            pltpu.VMEM((2, 2 * used, radial), f32),
            pltpu.VMEM((2, 2 * used, radial), f32),
            pltpu.VMEM((2, half, 2 * used, radial), f32),
            pltpu.VMEM((2, half, 2 * used, radial), f32),
            pltpu.SemaphoreType.DMA((4,)),
            pltpu.SemaphoreType.DMA((3, 2, 2, radial // CHUNK)),
            pltpu.SemaphoreType.DMA((3, 2, 2, radial // CHUNK)),
            pltpu.SemaphoreType.DMA((2,)),
            pltpu.SemaphoreType.DMA((2,)),
            pltpu.SemaphoreType.DMA((2, half)),
            pltpu.SemaphoreType.DMA((2, half)),
            pltpu.SemaphoreType.DMA((2,)),
            pltpu.SemaphoreType.DMA((2,)),
        ],
        compiler_params=pltpu.CompilerParams(
            collective_id=0, has_side_effects=True, vmem_limit_bytes=50 * 1024 * 1024
        ),
    )(mean_flow, offset, state_now, state_prev, eddy_visc)


def solution(mesh):
    placed = (
        P(None, None, "theta", "groups", None),
        P(None, None, "theta", "groups", None),
        P(None, "theta", "groups", None),
        P(),
        P("groups"),
    )
    return jax.shard_map(
        per_device,
        mesh=mesh,
        in_specs=placed,
        out_specs=P(None, None, "theta", "groups", None),
        check_vma=False,
    )
```

```python
import functools
import jax
import jax.numpy as jnp
from jax import lax
from jax.experimental import pallas as pl
from jax.experimental.pallas import tpu as pltpu
from jax.sharding import PartitionSpec as P

ITERS = 2
PSEUDO_STEP = 0.2
PHYS_STEP = 1.0
SECTIONS = 3
WEIGHT_EARLY = 0.6
WEIGHT_LAST = 1.0
PAD = 8
CHUNK = 64
MESH = pl.DeviceIdType.MESH
FAR, NEAR = 0, 1


def slot_of(s):
    r = lax.rem(s, SECTIONS)
    it = lax.rem(lax.div(s, SECTIONS), 2)
    return r + it * (1 - 2 * r + 3 * lax.div(r, 2))


def kernel(
    count, cells, radial,
    mean_ref, offset_ref, now_ref, prev_ref, eddy_hbm,
    out_ref,
    fbuf, fixed, eddy_ref, stage, gcol, packed, edge_eddy, eddy_send, eddy_recv,
    choose, plane, plane_recv, picks, got,
    load_sem, hsend, hrecv, xsend, xrecv, gsend, grecv, esend, erecv,
):
    me = lax.axis_index("theta")
    core = lax.rem(me, 2)
    cross = lax.rem(lax.div(me, 2), 2)
    half = count // 2
    rank = lax.div(me, 4) * 2 + core
    total = ITERS * SECTIONS
    width = fbuf.shape[-1]
    used = 5 * cells
    window = 5 * (cells + 2)
    block = edge_eddy.shape[1]
    circle = cells * count
    f32 = jnp.float32

    def at(index):
        return {"theta": lax.rem(index + count, count)}

    def same_side(j):
        other = lax.rem(rank + j, half)
        return lax.div(other, 2) * 4 + cross * 2 + lax.rem(other, 2)

    partner = at(me + 2 - 4 * cross)

    def after(side):
        return core + side * (1 - 2 * core)

    def peer(side):
        return at(me + 2 * after(side) - 1)

    def edge_layer(side):
        return 1 + after(side) * (cells - 1)

    def halo_layer(side):
        return after(side) * (cells + 1)

    loads = [
        pltpu.make_async_copy(
            now_ref, fbuf.at[0, :, :, pl.ds(1, cells), pl.ds(PAD, radial)], load_sem.at[0]
        ),
        pltpu.make_async_copy(prev_ref, fixed, load_sem.at[1]),
        pltpu.make_async_copy(eddy_hbm, eddy_ref, load_sem.at[2]),
    ]
    for load in loads:
        load.start()

    barrier = pltpu.get_barrier_semaphore()
    greet = [peer(FAR), partner] + [at(same_side(j)) for j in range(1, half)]
    for device in greet:
        pl.semaphore_signal(barrier, inc=1, device_id=device, device_id_type=MESH)
    pl.semaphore_wait(barrier, len(greet))

    def halo(slot, row, side, piece, first=False):
        r0 = piece * CHUNK if isinstance(piece, int) else pl.multiple_of(piece * CHUNK, CHUNK)
        if first:
            source = now_ref.at[:, row, edge_layer(side) - 1, pl.ds(r0, CHUNK)]
        else:
            source = stage.at[row, side, :, pl.ds(r0, CHUNK)]
        return pltpu.make_async_remote_copy(
            src_ref=source,
            dst_ref=fbuf.at[slot, :, row, halo_layer(1 - side), pl.ds(PAD + r0, CHUNK)],
            send_sem=hsend.at[slot, row, side, piece],
            recv_sem=hrecv.at[slot, row, side, piece],
            device_id=peer(side),
            device_id_type=MESH,
        )

    def cross_plane(par):
        return pltpu.make_async_remote_copy(
            src_ref=plane.at[par],
            dst_ref=plane_recv.at[par],
            send_sem=xsend.at[par],
            recv_sem=xrecv.at[par],
            device_id=partner,
            device_id_type=MESH,
        )

    def spread(par, j):
        return pltpu.make_async_remote_copy(
            src_ref=picks.at[par, j],
            dst_ref=got.at[par, rank],
            send_sem=gsend.at[par, j],
            recv_sem=grecv.at[par, j],
            device_id=at(same_side(j)),
            device_id_type=MESH,
        )

    def edge_of(side):
        return pltpu.make_async_remote_copy(
            src_ref=eddy_send,
            dst_ref=eddy_recv.at[side],
            send_sem=esend.at[side],
            recv_sem=erecv.at[side],
            device_id=peer(side),
            device_id_type=MESH,
        )

    for row in range(2):
        for side in (FAR, NEAR):
            for piece in range(radial // CHUNK):
                halo(0, row, side, piece, True).start()

    inverse = [(1.0 / jnp.full((8, width), mean_ref[row, 2], f32))[0, 0] for row in range(2)]
    shift = lax.rem(offset_ref[0], circle)
    start = [lax.rem(2 * circle - shift - 1, circle), lax.rem(circle + shift - 1, circle)]
    sector = [lax.div(value, cells) for value in start]
    within = [lax.rem(value, cells) for value in start]

    rows = lax.broadcasted_iota(jnp.int32, (2 * used, width), 0)
    is_stator = rows >= used
    is_end = lax.rem(lax.div(rows, 5), cells) == cells - 1

    def whether(target, part):
        apart = lax.rem(me - target - sector[part] + 2 * count, count)
        early = jnp.where(apart < 2, 1, 0)
        late = jnp.where(apart == 1, 1, jnp.where(apart == 2, 1, 0))
        return early, jnp.where(within[part] == cells - 1, late, early)

    for j in range(half):
        ends, rest = zip(*[whether(same_side(j), part) for part in range(2)])
        choose[j] = jnp.where(
            is_stator,
            jnp.where(is_end, ends[1], rest[1]),
            jnp.where(is_end, ends[0], rest[0]),
        )

    lane = lax.broadcasted_iota(jnp.int32, (CHUNK, width), 1)
    is_first = lane == 0
    is_last = lane == width - 1
    edge_lane = (width - 1, 0)
    edge_mask = (is_last, is_first)

    def place(acc, value, row, j):
        return jnp.where(lane == j, pltpu.roll(value, (j - edge_lane[row]) % width, 1), acc)

    def ghosts(slot):
        for row in range(2):
            for t in range(1, cells + 1):
                low = [fbuf[slot, c, row, t, pl.ds(PAD, 1), :] for c in range(5)]
                high = [fbuf[slot, c, row, t, pl.ds(PAD + radial - 1, 1), :] for c in range(5)]
                for c in range(5):
                    sign = -1.0 if c == 3 else 1.0
                    fbuf[slot, c, row, t, pl.ds(PAD - 1, 1), :] = sign * low[c]
                    fbuf[slot, c, row, t, pl.ds(PAD + radial, 1), :] = sign * high[c]

    def send_planes(par, own=None):
        lines = packed[...].T[: 2 * used]
        plane[par] = lines if own is None else lines + own
        cross_plane(par).start()

    def answer(par):
        cross_plane(par).wait()
        mine = plane[par]
        theirs = plane_recv[par]
        for j in range(half):
            picked = jnp.where(choose[j] > 0, mine, theirs)
            if j == 0:
                got[par, rank] = picked
            else:
                picks[par, j] = picked
                spread(par, j).start()

    def facing(par, part):
        parts = []
        for n in range(3):
            where = lax.rem(me + sector[part] + n, count)
            index = lax.div(where, 4) * 2 + lax.rem(where, 2)
            value = got[par, 0]
            for m in range(1, half):
                value = jnp.where(index == m, got[par, m], value)
            parts.append(value[part * used : (part + 1) * used])
        joined = jnp.concatenate(parts, axis=0)
        out = joined[:window]
        for m in range(1, cells):
            out = jnp.where(within[part] == m, joined[5 * m : 5 * m + window], out)
        return out

    component = lax.rem(lax.broadcasted_iota(jnp.int32, (window, width), 0), 5)

    def columns_of(par, k):
        pieces = []
        own = []
        for row in range(2):
            ghost = facing(par, 1 - row)
            half_k = (0.5 if row == 0 else -0.5) * k
            density, sound = mean_ref[row, 2], mean_ref[row, 3]
            up1 = jnp.concatenate([ghost[1:], ghost[:1]], axis=0)
            up3 = jnp.concatenate([ghost[3:], ghost[:3]], axis=0)
            down3 = jnp.concatenate([ghost[-3:], ghost[:-3]], axis=0)
            delta = (edge_eddy[row][:window] * k - mean_ref[row, 0] * half_k) * ghost
            push = jnp.where(
                component == 0,
                (density * half_k) * up1,
                jnp.where(
                    component == 1,
                    (inverse[row] * half_k) * up3,
                    jnp.where(component == 4, (density * sound * sound * half_k) * down3, 0.0),
                ),
            )
            delta = delta - push
            own.append(delta[5 : 5 + used])
            pieces.append(delta)
            pieces.append(jnp.zeros((block - window, width), f32))
        pieces.append(jnp.zeros((width - 2 * block, width), f32))
        gcol[par] = jnp.concatenate(pieces, axis=0).T
        return jnp.concatenate(own, axis=0)

    def patch_piece(slot, row, t, i, par):
        r0 = pl.multiple_of(i * CHUNK, CHUNK)
        columns = gcol[par, pl.ds(r0, CHUNK), :]
        new = []
        for c in range(5):
            amount = edge_lane[row] - row * block - t * 5 - c
            amount = amount % width if isinstance(t, int) else lax.rem(amount + 2 * width, width)
            moved = pltpu.roll(columns, amount, 1)
            value = fbuf[slot, c, row, t, pl.ds(r0 + PAD, CHUNK), :]
            new.append(value + jnp.where(edge_mask[row], moved, 0.0))
        for c in range(5):
            fbuf[slot, c, row, t, pl.ds(r0 + PAD, CHUNK), :] = new[c]

    def patch(slot, layers, par):
        def body(i, carry):
            for row, t in layers:
                patch_piece(slot, row, t, i, par)
            return carry

        lax.fori_loop(0, radial // CHUNK, body, 0)

    def pack(slot, layers, fresh):
        def body(i, carry):
            r0 = pl.multiple_of(i * CHUNK, CHUNK)
            acc = jnp.zeros((CHUNK, width), f32) if fresh else packed[pl.ds(r0, CHUNK), :]
            for row, t in layers:
                for c in range(5):
                    value = fbuf[slot, c, row, t, pl.ds(r0 + PAD, CHUNK), :]
                    acc = place(acc, value, row, row * used + (t - 1) * 5 + c)
            packed[pl.ds(r0, CHUNK), :] = acc
            return carry

        lax.fori_loop(0, radial // CHUNK, body, 0)

    def layer_piece(cur, new, origin, row, t, k, i, side=None):
        half_u = mean_ref[row, 0] * (0.5 * k)
        half_v = mean_ref[row, 1] * (0.5 * k)
        push_rho = mean_ref[row, 2] * (0.5 * k)
        push_inv = inverse[row] * (0.5 * k)
        push_p = mean_ref[row, 2] * mean_ref[row, 3] * mean_ref[row, 3] * (0.5 * k)

        r0 = pl.multiple_of(i * CHUNK, CHUNK)
        ke = eddy_ref[row, t - 1, pl.ds(r0, CHUNK), :] * k
        cf = ke * 6.0 + (1.5 / PHYS_STEP) * k
        partial = []
        extra = {}
        div = None
        for c in range(5):
            f = fbuf[cur, c, row, t, pl.ds(r0 + PAD, CHUNK), :]
            rm = fbuf[cur, c, row, t, pl.ds(r0 + (PAD - 1), CHUNK), :]
            rp = fbuf[cur, c, row, t, pl.ds(r0 + (PAD + 1), CHUNK), :]
            tm = fbuf[cur, c, row, t - 1, pl.ds(r0 + PAD, CHUNK), :]
            tp = fbuf[cur, c, row, t + 1, pl.ds(r0 + PAD, CHUNK), :]
            am = jnp.where(is_first, 0.0, pltpu.roll(f, 1, 1))
            ap = jnp.where(is_last, 0.0 if row == 0 else f, pltpu.roll(f, width - 1, 1))
            da = ap - am
            dt = tp - tm
            around = (ap + am) + (tp + tm) + (rp + rm)
            value = (
                fbuf[origin, c, row, t, pl.ds(r0 + PAD, CHUNK), :]
                - k * fixed[c, row, t - 1, pl.ds(r0, CHUNK), :]
                - cf * f
                + ke * around
                - half_u * da
                - half_v * dt
            )
            if c == 1:
                div = da
            elif c == 2:
                div = div + dt
            elif c == 3:
                div = div + (rp - rm)
            elif c == 4:
                extra = {1: da, 2: dt, 3: rp - rm}
            partial.append(value)
        for c in range(5):
            if c == 0:
                value = partial[0] - push_rho * div
            elif c == 4:
                value = partial[4] - push_p * div
            else:
                value = partial[c] - push_inv * extra[c]
            fbuf[new, c, row, t, pl.ds(r0 + PAD, CHUNK), :] = value
            if side is not None:
                stage[row, side, c, pl.ds(r0, CHUNK), :] = value

    def layer(cur, new, origin, row, t, k):
        def body(i, carry):
            layer_piece(cur, new, origin, row, t, k, i)
            return carry

        lax.fori_loop(0, radial // CHUNK, body, 0)

    loads[2].wait()

    def eddy_columns(i, carry):
        r0 = pl.multiple_of(i * CHUNK, CHUNK)
        acc = jnp.zeros((CHUNK, width), f32)
        for row in range(2):
            for t in range(cells):
                acc = place(acc, eddy_ref[row, t, pl.ds(r0, CHUNK), :], row, row * cells + t)
        packed[pl.ds(r0, CHUNK), :] = acc
        return carry

    lax.fori_loop(0, radial // CHUNK, eddy_columns, 0)
    eddy_send[...] = packed[...].T[: 2 * cells]
    for side in (FAR, NEAR):
        edge_of(side).start()
    loads[0].wait()
    rotor = [(0, t) for t in range(1, cells + 1)]
    stator_inner = [(1, t) for t in range(2, cells)]
    stator_edges = [(1, t) for t in sorted({1, cells})]
    pack(0, rotor + stator_inner + stator_edges, True)
    send_planes(0)
    ghosts(0)
    gcol[...] = jnp.zeros_like(gcol)
    loads[1].wait()

    def prepare(t, carry):
        for c in range(5):
            for row in range(2):
                fixed[c, row, t] = (0.5 / PHYS_STEP) * fixed[c, row, t] - (
                    2.0 / PHYS_STEP
                ) * fbuf[0, c, row, t + 1, pl.ds(PAD, radial), :]
        return carry

    lax.fori_loop(0, cells, prepare, 0)
    def join_eddy():
        for side in (FAR, NEAR):
            edge_of(side).wait()
        left = jnp.where(core == 0, eddy_recv[FAR], eddy_recv[NEAR])
        right = jnp.where(core == 0, eddy_recv[NEAR], eddy_recv[FAR])
        for row in range(2):
            own = eddy_send[...]
            line = [left[(row + 1) * cells - 1 : (row + 1) * cells]]
            line += [own[row * cells + t : row * cells + t + 1] for t in range(cells)]
            line += [right[row * cells : row * cells + 1]]
            edge_eddy[row] = jnp.concatenate(
                [jnp.broadcast_to(value, (5, width)) for value in line]
                + [jnp.zeros((block - window, width), f32)],
                axis=0,
            )

    def stores(chosen):
        pieces = [(0, 1, cells), (1, 2, cells - 2), (1, 1, 1), (1, cells, 1)]
        return [
            pltpu.make_async_copy(
                fbuf.at[0, :, row, pl.ds(t, n), pl.ds(PAD, radial)],
                out_ref.at[:, row, pl.ds(t - 1, n)],
                load_sem.at[index],
            )
            for index, (row, t, n) in enumerate(pieces)
            if index in chosen
        ]

    def section(s, carry):
        cur = slot_of(s)
        new = slot_of(s + 1)
        origin = lax.div(s, SECTIONS)
        par = lax.rem(s, 2)
        k = jnp.where(
            lax.rem(s, SECTIONS) == SECTIONS - 1,
            f32(WEIGHT_LAST * PSEUDO_STEP),
            f32(WEIGHT_EARLY * PSEUDO_STEP),
        )
        final = lax.div(s, total - 1)

        def edges(row):
            for n in range(2):
                side = n + final * (1 - 2 * n)

                def one(i, carry):
                    halo(cur, row, side, i).wait()
                    patch_piece(cur, row, halo_layer(side), i, 1 - par)
                    layer_piece(cur, new, origin, row, edge_layer(side), k, i, side)

                    @pl.when(s < total - 1)
                    def _():
                        halo(new, row, side, i).start()

                    return carry

                lax.fori_loop(0, radial // CHUNK, one, 0)

        def inside(row):
            def inner(t, carry):
                layer(cur, new, origin, row, t, k)
                return carry

            lax.fori_loop(2, cells, inner, 0)

        def take():
            for j in range(1, half):
                spread(par, j).wait()

            @pl.when(s == 0)
            def _():
                join_eddy()

            return columns_of(par, k)

        edges(0)
        answer(par)
        inside(0)
        pack(new, rotor, True)

        @pl.when(s == total - 1)
        def _():
            inside(1)

        edges(1)

        @pl.when(s < total - 1)
        def _():
            inside(1)
            pack(new, stator_inner + stator_edges, False)
            send_planes(1 - par, take())
            patch(new, rotor + stator_inner + stator_edges, par)
            ghosts(new)

        @pl.when(s == total - 1)
        def _():
            take()
            patch(new, rotor, par)
            stores((0,))[0].start()
            patch(new, stator_inner, par)
            stores((1,))[0].start()

        return carry

    lax.fori_loop(0, total, section, 0)
    for n, place_of in enumerate(stator_edges):
        patch(0, [place_of], (total - 1) % 2)
        stores((2 + n,))[0].start()
    for store in stores(range(4)):
        store.wait()


def per_device(state_now, state_prev, eddy_visc, mean_flow, offset):
    _, _, cells, radial, width = state_now.shape
    count = lax.axis_size("theta")
    half = count // 2
    block = -(-5 * (cells + 2) // 8) * 8
    used = 5 * cells
    f32 = jnp.float32
    hbm = pl.BlockSpec(memory_space=pltpu.HBM)
    smem = pl.BlockSpec(memory_space=pltpu.SMEM)
    return pl.pallas_call(
        functools.partial(kernel, count, cells, radial),
        out_shape=jax.ShapeDtypeStruct(state_now.shape, f32),
        in_specs=[smem, smem, hbm, hbm, hbm],
        out_specs=pl.BlockSpec(memory_space=pltpu.VMEM),
        scratch_shapes=[
            pltpu.VMEM((3, 5, 2, cells + 2, radial + 2 * PAD, width), f32),
            pltpu.VMEM((5, 2, cells, radial, width), f32),
            pltpu.VMEM((2, cells, radial, width), f32),
            pltpu.VMEM((2, 2, 5, radial, width), f32),
            pltpu.VMEM((2, radial, width), f32),
            pltpu.VMEM((radial, width), f32),
            pltpu.VMEM((2, block, radial), f32),
            pltpu.VMEM((2 * cells, radial), f32),
            pltpu.VMEM((2, 2 * cells, radial), f32),
            pltpu.VMEM((half, 2 * used, radial), jnp.int32),
            pltpu.VMEM((2, 2 * used, radial), f32),
            pltpu.VMEM((2, 2 * used, radial), f32),
            pltpu.VMEM((2, half, 2 * used, radial), f32),
            pltpu.VMEM((2, half, 2 * used, radial), f32),
            pltpu.SemaphoreType.DMA((4,)),
            pltpu.SemaphoreType.DMA((3, 2, 2, radial // CHUNK)),
            pltpu.SemaphoreType.DMA((3, 2, 2, radial // CHUNK)),
            pltpu.SemaphoreType.DMA((2,)),
            pltpu.SemaphoreType.DMA((2,)),
            pltpu.SemaphoreType.DMA((2, half)),
            pltpu.SemaphoreType.DMA((2, half)),
            pltpu.SemaphoreType.DMA((2,)),
            pltpu.SemaphoreType.DMA((2,)),
        ],
        compiler_params=pltpu.CompilerParams(
            collective_id=0, has_side_effects=True, vmem_limit_bytes=50 * 1024 * 1024
        ),
    )(mean_flow, offset, state_now, state_prev, eddy_visc)


def solution(mesh):
    placed = (
        P(None, None, "theta", "groups", None),
        P(None, None, "theta", "groups", None),
        P(None, "theta", "groups", None),
        P(),
        P("groups"),
    )
    return jax.shard_map(
        per_device,
        mesh=mesh,
        in_specs=placed,
        out_specs=P(None, None, "theta", "groups", None),
        check_vma=False,
    )
```

```python
import functools
import jax
import jax.numpy as jnp
from jax import lax
from jax.experimental import pallas as pl
from jax.experimental.pallas import tpu as pltpu
from jax.sharding import PartitionSpec as P

ITERS = 2
PSEUDO_STEP = 0.2
PHYS_STEP = 1.0
SECTIONS = 3
WEIGHT_EARLY = 0.6
WEIGHT_LAST = 1.0
PAD = 8
CHUNK = 64
MESH = pl.DeviceIdType.MESH
FAR, NEAR = 0, 1


def slot_of(s):
    r = lax.rem(s, SECTIONS)
    it = lax.rem(lax.div(s, SECTIONS), 2)
    return r + it * (1 - 2 * r + 3 * lax.div(r, 2))


def kernel(
    count, cells, radial,
    mean_ref, offset_ref, now_ref, prev_ref, eddy_hbm,
    out_ref,
    fbuf, fixed, eddy_ref, stage, gcol, packed, edge_eddy, eddy_send, eddy_recv,
    choose, plane, plane_recv, picks, got,
    load_sem, hsend, hrecv, xsend, xrecv, gsend, grecv, esend, erecv,
):
    me = lax.axis_index("theta")
    core = lax.rem(me, 2)
    cross = lax.rem(lax.div(me, 2), 2)
    half = count // 2
    rank = lax.div(me, 4) * 2 + core
    total = ITERS * SECTIONS
    width = fbuf.shape[-1]
    used = 5 * cells
    window = 5 * (cells + 2)
    block = edge_eddy.shape[1]
    circle = cells * count
    f32 = jnp.float32

    def at(index):
        return {"theta": lax.rem(index + count, count)}

    def same_side(j):
        other = lax.rem(rank + j, half)
        return lax.div(other, 2) * 4 + cross * 2 + lax.rem(other, 2)

    partner = at(me + 2 - 4 * cross)

    def after(side):
        return core + side * (1 - 2 * core)

    def peer(side):
        return at(me + 2 * after(side) - 1)

    def edge_layer(side):
        return 1 + after(side) * (cells - 1)

    def halo_layer(side):
        return after(side) * (cells + 1)

    loads = [
        pltpu.make_async_copy(
            now_ref, fbuf.at[0, :, :, pl.ds(1, cells), pl.ds(PAD, radial)], load_sem.at[0]
        ),
        pltpu.make_async_copy(prev_ref, fixed, load_sem.at[1]),
        pltpu.make_async_copy(eddy_hbm, eddy_ref, load_sem.at[2]),
    ]
    for load in loads:
        load.start()

    barrier = pltpu.get_barrier_semaphore()
    greet = [peer(FAR), partner] + [at(same_side(j)) for j in range(1, half)]
    for device in greet:
        pl.semaphore_signal(barrier, inc=1, device_id=device, device_id_type=MESH)
    pl.semaphore_wait(barrier, len(greet))

    def halo(slot, row, side, piece, first=False):
        r0 = piece * CHUNK if isinstance(piece, int) else pl.multiple_of(piece * CHUNK, CHUNK)
        if first:
            source = now_ref.at[:, row, edge_layer(side) - 1, pl.ds(r0, CHUNK)]
        else:
            source = stage.at[row, side, :, pl.ds(r0, CHUNK)]
        return pltpu.make_async_remote_copy(
            src_ref=source,
            dst_ref=fbuf.at[slot, :, row, halo_layer(1 - side), pl.ds(PAD + r0, CHUNK)],
            send_sem=hsend.at[slot, row, side, piece],
            recv_sem=hrecv.at[slot, row, side, piece],
            device_id=peer(side),
            device_id_type=MESH,
        )

    def cross_plane(par):
        return pltpu.make_async_remote_copy(
            src_ref=plane.at[par],
            dst_ref=plane_recv.at[par],
            send_sem=xsend.at[par],
            recv_sem=xrecv.at[par],
            device_id=partner,
            device_id_type=MESH,
        )

    def spread(par, j):
        return pltpu.make_async_remote_copy(
            src_ref=picks.at[par, j],
            dst_ref=got.at[par, rank],
            send_sem=gsend.at[par, j],
            recv_sem=grecv.at[par, j],
            device_id=at(same_side(j)),
            device_id_type=MESH,
        )

    def edge_of(side):
        return pltpu.make_async_remote_copy(
            src_ref=eddy_send,
            dst_ref=eddy_recv.at[side],
            send_sem=esend.at[side],
            recv_sem=erecv.at[side],
            device_id=peer(side),
            device_id_type=MESH,
        )

    for row in range(2):
        for side in (FAR, NEAR):
            for piece in range(radial // CHUNK):
                halo(0, row, side, piece, True).start()

    inverse = [(1.0 / jnp.full((8, width), mean_ref[row, 2], f32))[0, 0] for row in range(2)]
    shift = lax.rem(offset_ref[0], circle)
    start = [lax.rem(2 * circle - shift - 1, circle), lax.rem(circle + shift - 1, circle)]
    sector = [lax.div(value, cells) for value in start]
    within = [lax.rem(value, cells) for value in start]

    rows = lax.broadcasted_iota(jnp.int32, (2 * used, width), 0)
    is_stator = rows >= used
    is_end = lax.rem(lax.div(rows, 5), cells) == cells - 1

    def whether(target, part):
        apart = lax.rem(me - target - sector[part] + 2 * count, count)
        early = jnp.where(apart < 2, 1, 0)
        late = jnp.where(apart == 1, 1, jnp.where(apart == 2, 1, 0))
        return early, jnp.where(within[part] == cells - 1, late, early)

    for j in range(half):
        ends, rest = zip(*[whether(same_side(j), part) for part in range(2)])
        choose[j] = jnp.where(
            is_stator,
            jnp.where(is_end, ends[1], rest[1]),
            jnp.where(is_end, ends[0], rest[0]),
        )

    lane = lax.broadcasted_iota(jnp.int32, (CHUNK, width), 1)
    is_first = lane == 0
    is_last = lane == width - 1
    edge_lane = (width - 1, 0)
    edge_mask = (is_last, is_first)

    def place(acc, value, row, j):
        return jnp.where(lane == j, pltpu.roll(value, (j - edge_lane[row]) % width, 1), acc)

    def ghosts(slot):
        for row in range(2):
            for t in range(1, cells + 1):
                low = [fbuf[slot, c, row, t, pl.ds(PAD, 1), :] for c in range(5)]
                high = [fbuf[slot, c, row, t, pl.ds(PAD + radial - 1, 1), :] for c in range(5)]
                for c in range(5):
                    sign = -1.0 if c == 3 else 1.0
                    fbuf[slot, c, row, t, pl.ds(PAD - 1, 1), :] = sign * low[c]
                    fbuf[slot, c, row, t, pl.ds(PAD + radial, 1), :] = sign * high[c]

    def send_planes(par, own=None):
        lines = packed[...].T[: 2 * used]
        plane[par] = lines if own is None else lines + own
        cross_plane(par).start()

    def answer(par):
        cross_plane(par).wait()
        mine = plane[par]
        theirs = plane_recv[par]
        for j in range(half):
            picked = jnp.where(choose[j] > 0, mine, theirs)
            if j == 0:
                got[par, rank] = picked
            else:
                picks[par, j] = picked
                spread(par, j).start()

    def facing(par, part):
        parts = []
        for n in range(3):
            where = lax.rem(me + sector[part] + n, count)
            index = lax.div(where, 4) * 2 + lax.rem(where, 2)
            value = got[par, 0]
            for m in range(1, half):
                value = jnp.where(index == m, got[par, m], value)
            parts.append(value[part * used : (part + 1) * used])
        joined = jnp.concatenate(parts, axis=0)
        out = joined[:window]
        for m in range(1, cells):
            out = jnp.where(within[part] == m, joined[5 * m : 5 * m + window], out)
        return out

    component = lax.rem(lax.broadcasted_iota(jnp.int32, (window, width), 0), 5)

    def columns_of(par, k):
        pieces = []
        own = []
        for row in range(2):
            ghost = facing(par, 1 - row)
            half_k = (0.5 if row == 0 else -0.5) * k
            density, sound = mean_ref[row, 2], mean_ref[row, 3]
            up1 = jnp.concatenate([ghost[1:], ghost[:1]], axis=0)
            up3 = jnp.concatenate([ghost[3:], ghost[:3]], axis=0)
            down3 = jnp.concatenate([ghost[-3:], ghost[:-3]], axis=0)
            delta = (edge_eddy[row][:window] * k - mean_ref[row, 0] * half_k) * ghost
            push = jnp.where(
                component == 0,
                (density * half_k) * up1,
                jnp.where(
                    component == 1,
                    (inverse[row] * half_k) * up3,
                    jnp.where(component == 4, (density * sound * sound * half_k) * down3, 0.0),
                ),
            )
            delta = delta - push
            own.append(delta[5 : 5 + used])
            pieces.append(delta)
            pieces.append(jnp.zeros((block - window, width), f32))
        pieces.append(jnp.zeros((width - 2 * block, width), f32))
        gcol[par] = jnp.concatenate(pieces, axis=0).T
        return jnp.concatenate(own, axis=0)

    def patch_piece(slot, row, t, i, par):
        r0 = pl.multiple_of(i * CHUNK, CHUNK)
        columns = gcol[par, pl.ds(r0, CHUNK), :]
        new = []
        for c in range(5):
            amount = edge_lane[row] - row * block - t * 5 - c
            amount = amount % width if isinstance(t, int) else lax.rem(amount + 2 * width, width)
            moved = pltpu.roll(columns, amount, 1)
            value = fbuf[slot, c, row, t, pl.ds(r0 + PAD, CHUNK), :]
            new.append(value + jnp.where(edge_mask[row], moved, 0.0))
        for c in range(5):
            fbuf[slot, c, row, t, pl.ds(r0 + PAD, CHUNK), :] = new[c]

    def patch_out(layers, par):
        def body(i, carry):
            r0 = pl.multiple_of(i * CHUNK, CHUNK)
            columns = gcol[par, pl.ds(r0, CHUNK), :]
            for row, t in layers:
                new = []
                for c in range(5):
                    amount = (edge_lane[row] - row * block - t * 5 - c) % width
                    moved = jnp.where(edge_mask[row], pltpu.roll(columns, amount, 1), 0.0)
                    new.append(out_ref[c, row, t - 1, pl.ds(r0, CHUNK), :] + moved)
                for c in range(5):
                    out_ref[c, row, t - 1, pl.ds(r0, CHUNK), :] = new[c]
            return carry

        lax.fori_loop(0, radial // CHUNK, body, 0)

    def patch(slot, layers, par):
        def body(i, carry):
            for row, t in layers:
                patch_piece(slot, row, t, i, par)
            return carry

        lax.fori_loop(0, radial // CHUNK, body, 0)

    def pack(slot, layers, fresh):
        def body(i, carry):
            r0 = pl.multiple_of(i * CHUNK, CHUNK)
            acc = jnp.zeros((CHUNK, width), f32) if fresh else packed[pl.ds(r0, CHUNK), :]
            for row, t in layers:
                for c in range(5):
                    value = fbuf[slot, c, row, t, pl.ds(r0 + PAD, CHUNK), :]
                    acc = place(acc, value, row, row * used + (t - 1) * 5 + c)
            packed[pl.ds(r0, CHUNK), :] = acc
            return carry

        lax.fori_loop(0, radial // CHUNK, body, 0)

    def layer_piece(cur, new, origin, row, t, k, i, side=None):
        half_u = mean_ref[row, 0] * (0.5 * k)
        half_v = mean_ref[row, 1] * (0.5 * k)
        push_rho = mean_ref[row, 2] * (0.5 * k)
        push_inv = inverse[row] * (0.5 * k)
        push_p = mean_ref[row, 2] * mean_ref[row, 3] * mean_ref[row, 3] * (0.5 * k)

        r0 = pl.multiple_of(i * CHUNK, CHUNK)
        ke = eddy_ref[row, t - 1, pl.ds(r0, CHUNK), :] * k
        cf = ke * 6.0 + (1.5 / PHYS_STEP) * k
        partial = []
        extra = {}
        div = None
        for c in range(5):
            f = fbuf[cur, c, row, t, pl.ds(r0 + PAD, CHUNK), :]
            rm = fbuf[cur, c, row, t, pl.ds(r0 + (PAD - 1), CHUNK), :]
            rp = fbuf[cur, c, row, t, pl.ds(r0 + (PAD + 1), CHUNK), :]
            tm = fbuf[cur, c, row, t - 1, pl.ds(r0 + PAD, CHUNK), :]
            tp = fbuf[cur, c, row, t + 1, pl.ds(r0 + PAD, CHUNK), :]
            am = jnp.where(is_first, 0.0, pltpu.roll(f, 1, 1))
            ap = jnp.where(is_last, 0.0 if row == 0 else f, pltpu.roll(f, width - 1, 1))
            da = ap - am
            dt = tp - tm
            around = (ap + am) + (tp + tm) + (rp + rm)
            value = (
                fbuf[origin, c, row, t, pl.ds(r0 + PAD, CHUNK), :]
                - k * fixed[c, row, t - 1, pl.ds(r0, CHUNK), :]
                - cf * f
                + ke * around
                - half_u * da
                - half_v * dt
            )
            if c == 1:
                div = da
            elif c == 2:
                div = div + dt
            elif c == 3:
                div = div + (rp - rm)
            elif c == 4:
                extra = {1: da, 2: dt, 3: rp - rm}
            partial.append(value)
        for c in range(5):
            if c == 0:
                value = partial[0] - push_rho * div
            elif c == 4:
                value = partial[4] - push_p * div
            else:
                value = partial[c] - push_inv * extra[c]
            fbuf[new, c, row, t, pl.ds(r0 + PAD, CHUNK), :] = value
            if side is not None:
                stage[row, side, c, pl.ds(r0, CHUNK), :] = value

    def layer(cur, new, origin, row, t, k):
        def body(i, carry):
            layer_piece(cur, new, origin, row, t, k, i)
            return carry

        lax.fori_loop(0, radial // CHUNK, body, 0)

    loads[2].wait()

    def eddy_columns(i, carry):
        r0 = pl.multiple_of(i * CHUNK, CHUNK)
        acc = jnp.zeros((CHUNK, width), f32)
        for row in range(2):
            for t in range(cells):
                acc = place(acc, eddy_ref[row, t, pl.ds(r0, CHUNK), :], row, row * cells + t)
        packed[pl.ds(r0, CHUNK), :] = acc
        return carry

    lax.fori_loop(0, radial // CHUNK, eddy_columns, 0)
    eddy_send[...] = packed[...].T[: 2 * cells]
    for side in (FAR, NEAR):
        edge_of(side).start()
    loads[0].wait()
    rotor = [(0, t) for t in range(1, cells + 1)]
    stator_inner = [(1, t) for t in range(2, cells)]
    stator_edges = [(1, t) for t in sorted({1, cells})]
    pack(0, rotor + stator_inner + stator_edges, True)
    send_planes(0)
    ghosts(0)
    gcol[...] = jnp.zeros_like(gcol)
    loads[1].wait()

    def prepare(t, carry):
        for c in range(5):
            for row in range(2):
                fixed[c, row, t] = (0.5 / PHYS_STEP) * fixed[c, row, t] - (
                    2.0 / PHYS_STEP
                ) * fbuf[0, c, row, t + 1, pl.ds(PAD, radial), :]
        return carry

    lax.fori_loop(0, cells, prepare, 0)
    def join_eddy():
        for side in (FAR, NEAR):
            edge_of(side).wait()
        left = jnp.where(core == 0, eddy_recv[FAR], eddy_recv[NEAR])
        right = jnp.where(core == 0, eddy_recv[NEAR], eddy_recv[FAR])
        for row in range(2):
            own = eddy_send[...]
            line = [left[(row + 1) * cells - 1 : (row + 1) * cells]]
            line += [own[row * cells + t : row * cells + t + 1] for t in range(cells)]
            line += [right[row * cells : row * cells + 1]]
            edge_eddy[row] = jnp.concatenate(
                [jnp.broadcast_to(value, (5, width)) for value in line]
                + [jnp.zeros((block - window, width), f32)],
                axis=0,
            )

    def stores(chosen):
        pieces = [(0, 1, cells), (1, 2, cells - 2), (1, 1, 1), (1, cells, 1)]
        return [
            pltpu.make_async_copy(
                fbuf.at[0, :, row, pl.ds(t, n), pl.ds(PAD, radial)],
                out_ref.at[:, row, pl.ds(t - 1, n)],
                load_sem.at[index],
            )
            for index, (row, t, n) in enumerate(pieces)
            if index in chosen
        ]

    def section(s, carry):
        cur = slot_of(s)
        new = slot_of(s + 1)
        origin = lax.div(s, SECTIONS)
        par = lax.rem(s, 2)
        k = jnp.where(
            lax.rem(s, SECTIONS) == SECTIONS - 1,
            f32(WEIGHT_LAST * PSEUDO_STEP),
            f32(WEIGHT_EARLY * PSEUDO_STEP),
        )
        final = lax.div(s, total - 1)

        def edges(row):
            for n in range(2):
                side = n + final * (1 - 2 * n)

                def one(i, carry):
                    halo(cur, row, side, i).wait()
                    patch_piece(cur, row, halo_layer(side), i, 1 - par)
                    layer_piece(cur, new, origin, row, edge_layer(side), k, i, side)

                    @pl.when(s < total - 1)
                    def _():
                        halo(new, row, side, i).start()

                    return carry

                lax.fori_loop(0, radial // CHUNK, one, 0)

        def inside(row):
            def inner(t, carry):
                layer(cur, new, origin, row, t, k)
                return carry

            lax.fori_loop(2, cells, inner, 0)

        def take():
            for j in range(1, half):
                spread(par, j).wait()

            @pl.when(s == 0)
            def _():
                join_eddy()

            return columns_of(par, k)

        edges(0)
        answer(par)
        inside(0)
        pack(new, rotor, True)

        @pl.when(s == total - 1)
        def _():
            inside(1)
            for store in stores((0, 1)):
                store.start()

        edges(1)

        @pl.when(s < total - 1)
        def _():
            inside(1)
            pack(new, stator_inner + stator_edges, False)
            send_planes(1 - par, take())
            patch(new, rotor + stator_inner + stator_edges, par)
            ghosts(new)

        @pl.when(s == total - 1)
        def _():
            for store in stores((2, 3)):
                store.start()
            take()
            for store in stores((0, 1)):
                store.wait()
            patch_out(rotor + stator_inner, par)
            for store in stores((2, 3)):
                store.wait()
            patch_out(stator_edges, par)

        return carry

    lax.fori_loop(0, total, section, 0)


def per_device(state_now, state_prev, eddy_visc, mean_flow, offset):
    _, _, cells, radial, width = state_now.shape
    count = lax.axis_size("theta")
    half = count // 2
    block = -(-5 * (cells + 2) // 8) * 8
    used = 5 * cells
    f32 = jnp.float32
    hbm = pl.BlockSpec(memory_space=pltpu.HBM)
    smem = pl.BlockSpec(memory_space=pltpu.SMEM)
    return pl.pallas_call(
        functools.partial(kernel, count, cells, radial),
        out_shape=jax.ShapeDtypeStruct(state_now.shape, f32),
        in_specs=[smem, smem, hbm, hbm, hbm],
        out_specs=pl.BlockSpec(memory_space=pltpu.VMEM),
        scratch_shapes=[
            pltpu.VMEM((3, 5, 2, cells + 2, radial + 2 * PAD, width), f32),
            pltpu.VMEM((5, 2, cells, radial, width), f32),
            pltpu.VMEM((2, cells, radial, width), f32),
            pltpu.VMEM((2, 2, 5, radial, width), f32),
            pltpu.VMEM((2, radial, width), f32),
            pltpu.VMEM((radial, width), f32),
            pltpu.VMEM((2, block, radial), f32),
            pltpu.VMEM((2 * cells, radial), f32),
            pltpu.VMEM((2, 2 * cells, radial), f32),
            pltpu.VMEM((half, 2 * used, radial), jnp.int32),
            pltpu.VMEM((2, 2 * used, radial), f32),
            pltpu.VMEM((2, 2 * used, radial), f32),
            pltpu.VMEM((2, half, 2 * used, radial), f32),
            pltpu.VMEM((2, half, 2 * used, radial), f32),
            pltpu.SemaphoreType.DMA((4,)),
            pltpu.SemaphoreType.DMA((3, 2, 2, radial // CHUNK)),
            pltpu.SemaphoreType.DMA((3, 2, 2, radial // CHUNK)),
            pltpu.SemaphoreType.DMA((2,)),
            pltpu.SemaphoreType.DMA((2,)),
            pltpu.SemaphoreType.DMA((2, half)),
            pltpu.SemaphoreType.DMA((2, half)),
            pltpu.SemaphoreType.DMA((2,)),
            pltpu.SemaphoreType.DMA((2,)),
        ],
        compiler_params=pltpu.CompilerParams(
            collective_id=0, has_side_effects=True, vmem_limit_bytes=50 * 1024 * 1024
        ),
    )(mean_flow, offset, state_now, state_prev, eddy_visc)


def solution(mesh):
    placed = (
        P(None, None, "theta", "groups", None),
        P(None, None, "theta", "groups", None),
        P(None, "theta", "groups", None),
        P(),
        P("groups"),
    )
    return jax.shard_map(
        per_device,
        mesh=mesh,
        in_specs=placed,
        out_specs=P(None, None, "theta", "groups", None),
        check_vma=False,
    )
```
